32 devices in a mesh: sub: 2 (over x), col: 8 (over z, core), grp: 2 (over y).
Axes of the slice: x: 2, y: 2, z: 4, core: 2. Of those that a mesh axis runs over, the one named last changes fastest.
Arguments:
- first_rhs: float32 [2, 640, 1024], P('sub', None, 'col'), may hold values from -6 to 6
- innovations: float32 [2, 512, 640], P('sub', 'col'), may hold values from -6 to 6
- start_mult: float32 [2, 640, 1024], P('sub', None, 'col'), may hold values from -4 to 4
- trajectory: bfloat16 [2, 640, 1024], P('sub', None, 'col'), may hold values from -6 to 6
- weight_in: float32 [4096, 640], P('grp'), may hold values from -0.25 to 0.25
- weight_out: float32 [640, 4096], P(None, 'grp'), may hold values from -0.09375 to 0.09375
- vertical_modes: float32 [640, 640], P('grp'), may hold values from -0.25 to 0.25
- length_scale: float32 [640], replicated, may hold values from 1 to 8
- band_limit: int32 [640], replicated, may hold values from 1 to 128
- obs_col: int32 [2, 512], P('sub', 'col'), may hold values from 0 to 1023, as said below
- obs_count: int32 [2, 8], P('sub', 'col'), may hold values from 1 to 64
- obs_var: float32 [2, 512], P('sub', 'col'), may hold values from 0.25 to 4
Outputs:
- multiplier: float32 [2, 640, 1024], P('sub', None, 'col')
- obs_multiplier: float32 [2, 512, 640], P('sub', 'col')
- increment: float32 [2, 640, 1024], P('sub', None, 'col')
The draws below stay inside these ranges and needn't reach their ends.
Inputs may be any that keep to these rules, and one draw needn't show every extreme that they name: `obs_col`: slot j of a subwindow observes a column of shard j // 64: a column from (j // 64) * 128 to (j // 64 + 1) * 128 - 1.
All inputs are finite; a program needn't handle non-finite values.
Results may differ from the reference program's by a relative error of at most 0.0003.
Values sent between devices are 32-bit elements; how exact they have to be, the bound alone decides.
No kernel may reach another device: no remote copies, remote signals or barrier semaphores. Data moves between devices by JAX's collectives and lax.ppermute only.
A program may use at most 128 MiB of HBM per device.

```python
import math
import jax
import jax.numpy as jnp
from jax import lax

D = 640
HID = 4096
COLS_DEV = 128
OBS_DEV = 64
KW = 128
ITERS = 2
SUBS = 2
SHARDS = 8
COLS = 1024
SLOTS = 512


def draw_obs_col(key, part):
    offsets = jax.random.randint(key, (SUBS, SLOTS), 0, COLS_DEV)
    base = jnp.arange(SLOTS, dtype=jnp.int32) // OBS_DEV * COLS_DEV
    return (offsets + base[None, :]).astype(jnp.int32)


def touch_ends(result, key, smallest, top_value):
    index_at = [jax.random.randint(jax.random.fold_in(key, axis), (), 0, length) for axis, length in enumerate(result.shape)]
    longest = result.shape.index(max(result.shape))
    beside = index_at[:longest] + [(index_at[longest] + 1) % result.shape[longest]] + index_at[longest + 1:]
    return result.at[tuple(index_at)].set(smallest).at[tuple(beside)].set(top_value)


def levels(stream_key, shape, cuts, smallest, top_value):
    gain = 1.0
    for dim, blocks in cuts:
        steps = jax.random.uniform(jax.random.fold_in(jax.random.fold_in(stream_key, 6), dim), (blocks,), jnp.float32, smallest / len(cuts), top_value / len(cuts))
        gain = gain * jnp.repeat(jnp.exp(steps), shape[dim] // blocks).reshape((-1,) + (1,) * (len(shape) - 1 - dim))
    return gain


def scatter_about(stream_key, dims, scale, bound, cuts=(), held_as=jnp.bfloat16):
    loudness = levels(stream_key, dims, cuts, -0.22, 0.18) if cuts else 1.0
    result = jax.random.normal(stream_key, dims, jnp.float32) * scale * loudness
    return jnp.minimum(jnp.maximum(result, -bound), bound).astype(held_as)


def setup_inputs(seed: int = 0) -> dict:
    arg_keys = jax.random.split(jax.random.key(seed), 13)
    first_rhs = scatter_about(arg_keys[0], (SUBS, D, COLS), 1.0, 6.0, ((0, 2), (2, 8)), jnp.float32)
    innovations = scatter_about(arg_keys[1], (SUBS, SLOTS, D), 1.0, 6.0, ((0, 2), (1, 8)), jnp.float32)
    start_mult = scatter_about(arg_keys[2], (SUBS, D, COLS), 0.5, 4.0, ((0, 2), (2, 8)), jnp.float32)
    trajectory = scatter_about(arg_keys[3], (SUBS, D, COLS), 1.0, 6.0, ((0, 2), (2, 8)))
    weight_in = scatter_about(arg_keys[4], (HID, D), D ** -0.5, 0.25, ((0, 2),), jnp.float32)
    weight_out = scatter_about(arg_keys[5], (D, HID), HID ** -0.5, 0.09375, ((1, 2),), jnp.float32)
    vertical_modes = scatter_about(arg_keys[6], (D, D), D ** -0.5, 0.25, ((0, 2),), jnp.float32)
    length_scale = jnp.clip(jnp.exp(jax.random.uniform(arg_keys[7], (D,), jnp.float32, math.log(1.0), math.log(8.0))), 1.0, 8.0)
    band_limit = touch_ends(jax.random.randint(arg_keys[8], (D,), 1, KW + 1), jax.random.fold_in(arg_keys[8], 1), 1, KW).astype(jnp.int32)
    obs_col = draw_obs_col(jax.random.fold_in(arg_keys[12], 71), 0)
    obs_count = touch_ends(jax.random.randint(arg_keys[10], (SUBS, SHARDS), 1, OBS_DEV + 1), jax.random.fold_in(arg_keys[10], 1), 1, OBS_DEV).astype(jnp.int32)
    obs_var = jnp.clip(jnp.exp(math.log(4.0) - 2.7725887 * jax.random.uniform(arg_keys[11], (SUBS, SLOTS), jnp.float32) ** levels(arg_keys[11], (SUBS, SLOTS), ((0, 2), (1, 8)), -0.2, 0.2)), 0.25, 4.0)
    return dict(first_rhs=first_rhs, innovations=innovations, start_mult=start_mult, trajectory=trajectory, weight_in=weight_in, weight_out=weight_out, vertical_modes=vertical_modes, length_scale=length_scale, band_limit=band_limit, obs_col=obs_col, obs_count=obs_count, obs_var=obs_var)


HIGH = lax.Precision.HIGHEST


def spectral_table(columns, count, total):
    waves = jnp.arange(count, dtype=jnp.int32)
    phase = (columns[:, None] * waves[None, :]) % total
    angle = (2.0 * math.pi / total) * phase.astype(jnp.float32)
    return jnp.concatenate([jnp.cos(angle), jnp.sin(angle)], axis=1)


def spectrum(scales, limits, total, count):
    waves = jnp.arange(count, dtype=jnp.int32)
    wavef = waves.astype(jnp.float32)
    decay = jnp.exp(-0.5 * (2.0 * math.pi * wavef[None, :] * scales[:, None] / total) ** 2)
    factor = jnp.where(waves == 0, 1.0, 2.0).astype(jnp.float32) / total
    keep = (waves[None, :] < limits[:, None]).astype(jnp.float32)
    values = decay * factor[None, :] * keep
    return jnp.concatenate([values, values], axis=1)


def reference(first_rhs, innovations, start_mult, trajectory, weight_in, weight_out, vertical_modes, length_scale, band_limit, obs_col, obs_count, obs_var):
    slopes = 1.0 - jnp.tanh(jnp.einsum("hd,sdc->shc", weight_in, trajectory.astype(jnp.float32), precision=HIGH)) ** 2

    def tangent(field):
        inner = jnp.einsum("hd,sdc->shc", weight_in, field, precision=HIGH)
        return field + jnp.einsum("dh,shc->sdc", weight_out, slopes * inner, precision=HIGH)

    def adjoint(field):
        inner = jnp.einsum("dh,sdc->shc", weight_out, field, precision=HIGH)
        return field + jnp.einsum("hd,shc->sdc", weight_in, slopes * inner, precision=HIGH)

    def apply_lower(field):
        moved = tangent(field)[:-1]
        return field - jnp.concatenate([jnp.zeros_like(field[:1]), moved], axis=0)

    def apply_upper(field):
        later = jnp.concatenate([field[1:], jnp.zeros_like(field[:1])], axis=0)
        return field - adjoint(later)

    table = spectral_table(jnp.arange(COLS, dtype=jnp.int32), KW, COLS)
    spec = spectrum(length_scale, band_limit, COLS, KW)

    def covariance(field):
        modes = jnp.einsum("md,sdc->smc", vertical_modes, field, precision=HIGH)
        coeffs = jnp.einsum("smc,ck->smk", modes, table, precision=HIGH) * spec[None]
        back = jnp.einsum("smk,ck->smc", coeffs, table, precision=HIGH)
        return jnp.einsum("md,smc->sdc", vertical_modes, back, precision=HIGH)

    slot_ids = jnp.arange(SLOTS, dtype=jnp.int32)
    live = ((slot_ids % OBS_DEV)[None, :] < obs_count[:, slot_ids // OBS_DEV]).astype(jnp.float32)

    def observe(field):
        picked = jnp.take_along_axis(field, obs_col[:, None, :], axis=2)
        return jnp.transpose(picked, (0, 2, 1)) * live[:, :, None]

    def spread(values):
        masked = values * live[:, :, None]
        blank = jnp.zeros((SUBS, D, COLS), jnp.float32)
        return jax.vmap(lambda target, where_at, items: target.at[:, where_at].add(items.T))(blank, obs_col, masked)

    def later_sums(field):
        return jnp.flip(jnp.cumsum(jnp.flip(field, 0), axis=0), 0)

    def earlier_sums(field):
        return jnp.cumsum(field, axis=0)

    multiplier = start_mult
    obs_multiplier = jnp.zeros_like(innovations)
    increment = jnp.zeros_like(start_mult)
    res_mult = first_rhs - covariance(start_mult)
    res_obs = innovations
    res_state = -apply_upper(start_mult)
    for sweep in range(ITERS):
        dir_mult = later_sums(res_state)
        cov_mult = covariance(dir_mult)
        dir_state = earlier_sums(res_mult - cov_mult)
        dir_obs = res_obs / obs_var[:, :, None]
        image_mult = cov_mult + apply_lower(dir_state)
        image_obs = obs_var[:, :, None] * dir_obs + observe(dir_state)
        image_state = apply_upper(dir_mult) + spread(dir_obs)
        upper = jnp.sum(image_mult * res_mult) + jnp.sum(image_obs * res_obs) + jnp.sum(image_state * res_state)
        lower = jnp.sum(image_mult * image_mult) + jnp.sum(image_obs * image_obs) + jnp.sum(image_state * image_state)
        alpha = upper / lower
        multiplier = multiplier + alpha * dir_mult
        obs_multiplier = obs_multiplier + alpha * dir_obs
        increment = increment + alpha * dir_state
        res_mult = res_mult - alpha * image_mult
        res_obs = res_obs - alpha * image_obs
        res_state = res_state - alpha * image_state
    return multiplier, obs_multiplier, increment
```

```python
import math

import jax
import jax.numpy as jnp
import numpy as np
from jax import lax
from jax.sharding import PartitionSpec as P

KW = 128


HIGH = lax.Precision.HIGH


def contract(left, right, over):
    return lax.dot_general(
        left, right, ((over[:1], over[1:]), ((), ())), precision=HIGH, preferred_element_type=jnp.float32
    )


def product(left, right):
    return contract(left, right, (1, 0))


def product_first(left, right):
    return contract(left, right, (0, 0))


def spectral_table(columns, count, total):
    waves = jnp.arange(count, dtype=jnp.int32)
    phase = columns[:, None] * waves[None, :] % total
    angle = 2.0 * math.pi / total * phase.astype(jnp.float32)
    return jnp.concatenate([jnp.cos(angle), jnp.sin(angle)], axis=1)


def spectrum(scales, limits, total, count):
    waves = jnp.arange(count, dtype=jnp.int32)
    wavef = waves.astype(jnp.float32)
    decay = jnp.exp(-0.5 * (2.0 * math.pi * wavef[None, :] * scales[:, None] / total) ** 2)
    factor = jnp.where(waves == 0, 1.0, 2.0).astype(jnp.float32) / total
    keep = (waves[None, :] < limits[:, None]).astype(jnp.float32)
    values = decay * factor[None, :] * keep
    return jnp.concatenate([values, values], axis=1)


def rotated(block, axis, distance):
    size = lax.axis_size(axis)
    return lax.ppermute(block, axis, [(i, (i + distance) % size) for i in range(size)])


def mixtures(field, plans):
    size = lax.axis_size("sub")
    here = lax.axis_index("sub")
    masked = []
    for matrix, unread, zero in plans:
        weights = np.array(matrix, dtype=np.float32)
        live = np.ones_like(weights, dtype=bool)
        live[list(unread), :] = False
        live[:, list(zero)] = False
        masked.append((weights, live))
    arrived = {}
    for distance in range(1, size):
        route = [
            (source, (source + distance) % size)
            for source in range(size)
            if any(w[(source + distance) % size, source] * l[(source + distance) % size, source] for w, l in masked)
        ]
        if route:
            arrived[distance] = lax.ppermute(field, "sub", route)
    results = []
    for weights, live in masked:
        total = None
        for distance in range(size):
            cells = [(i, (i - distance) % size) for i in range(size)]
            used = {float(weights[c]) for c in cells if live[c]}
            if not used or used == {0.0}:
                continue
            block = field if distance == 0 else arrived[distance]
            if len(used) > 1:
                block = block * jnp.asarray([weights[c] for c in cells], jnp.float32)[here]
            elif used != {1.0}:
                block = block * used.pop()
            total = block if total is None else total + block
        results.append(total)
    return results


def plus(*terms):
    kept = [term for term in terms if term is not None]
    return sum(kept[1:], kept[0]) if kept else None


def on_device(
    first_rhs,
    innovations,
    start_mult,
    trajectory,
    weight_in,
    weight_out,
    vertical_modes,
    length_scale,
    band_limit,
    obs_col,
    obs_count,
    obs_var,
):
    rhs = first_rhs[0]
    data = innovations[0]
    start = start_mult[0]
    variance = obs_var[0][:, None]
    depth, width = rhs.shape
    subs = lax.axis_size("sub")
    shards = lax.axis_size("col")
    groups = lax.axis_size("grp")
    here = lax.axis_index("sub")
    column_index = lax.axis_index("col")
    group_index = lax.axis_index("grp")
    total_cols = width * shards
    half_modes = vertical_modes.shape[0]
    owned_modes = half_modes // shards
    rows = depth // groups

    ones = np.ones((subs, subs))
    up = np.eye(subs, k=1)
    down = np.eye(subs, k=-1)
    later = np.triu(ones)
    earlier = np.tril(ones)
    first = (0,)

    def own(field):
        return lax.dynamic_slice_in_dim(field, group_index * rows, rows, 0)

    def summed(partial):
        return sum((rotated(partial, "grp", step) for step in range(1, groups)), partial)

    def summed_own(partial):
        total = own(partial)
        for step in range(1, groups):
            target = (group_index + step) % groups
            total = total + rotated(
                lax.dynamic_slice_in_dim(partial, target * rows, rows, 0), "grp", step
            )
        return total

    def joined(block):
        whole = lax.dynamic_update_slice_in_dim(
            jnp.zeros((depth, block.shape[1]), block.dtype), block, group_index * rows, 0
        )
        for step in range(1, groups):
            source = (group_index - step) % groups
            whole = lax.dynamic_update_slice_in_dim(whole, rotated(block, "grp", step), source * rows, 0)
        return whole

    before = lax.ppermute(trajectory[0].astype(jnp.float32), "sub", [(i, i + 1) for i in range(subs - 1)])
    slopes = (1.0 - jnp.tanh(product(weight_in, before)) ** 2) * (here > 0).astype(jnp.float32)

    def side_by_side(*fields):
        return jnp.concatenate(fields, axis=1)

    def scaled(inner):
        return inner * jnp.tile(slopes, (1, inner.shape[1] // width))

    def tangent(fields):
        return product(weight_out, scaled(product(weight_in, fields)))

    def adjoint(fields):
        return product_first(weight_in, scaled(product_first(weight_out, fields)))

    first_mode = group_index * half_modes + column_index * owned_modes
    owned_scales = lax.dynamic_slice_in_dim(length_scale, first_mode, owned_modes, 0)
    owned_limits = lax.dynamic_slice_in_dim(band_limit, first_mode, owned_modes, 0)
    owned_spec = spectrum(owned_scales, owned_limits, total_cols, KW)
    table = spectral_table(jnp.arange(total_cols, dtype=jnp.int32), KW, total_cols)
    table_blocks = table.reshape(shards, width, 2 * KW)

    def covariance(fields):
        count = fields.shape[1] // width
        amplitudes = product(vertical_modes, fields).reshape(shards, owned_modes, count, width)
        owned = lax.all_to_all(amplitudes, "col", 0, 0, tiled=True)
        owned = owned.transpose(1, 2, 0, 3).reshape(owned_modes * count, total_cols)
        coeffs = product(owned, table).reshape(owned_modes, count, 2 * KW) * owned_spec[:, None, :]
        back = contract(coeffs.reshape(owned_modes * count, 2 * KW), table, (1, 1))
        back = back.reshape(owned_modes, count, shards, width).transpose(2, 0, 1, 3)
        returned = lax.all_to_all(back, "col", 0, 0, tiled=True)
        return product_first(vertical_modes, returned.reshape(half_modes, count * width))

    local_cols = obs_col[0] - column_index * width
    slot_ids = jnp.arange(local_cols.shape[0], dtype=jnp.int32)
    live = (slot_ids < obs_count[0, 0]).astype(jnp.float32)
    pick = (jnp.arange(width, dtype=jnp.int32)[:, None] == local_cols[None, :]).astype(jnp.float32) * live[None, :]

    def observe(field):
        return contract(pick, field, (0, 1))

    def spread(values):
        return contract(values, pick, (0, 1))

    dir_obs = data / variance
    obs_push = spread(dir_obs)

    push_fed, push_later = mixtures(obs_push, [(later, first, ()), (later, (), ())])
    pulled = adjoint(side_by_side(start, push_fed))
    pull0 = summed(pulled[:, :width])
    pull2 = summed_own(pulled[:, width:])
    pull0_fed, pull0_later = mixtures(pull0, [(later @ up, first, first), (later @ up, (), first)])
    pull1 = pull1_later = None
    if pull0_fed is not None:
        pull1 = summed(adjoint(pull0_fed))
        pull1_fed, pull1_later = mixtures(pull1, [(later @ up, first, first), (later @ up, (), first)])
        pull2 = pull2 + own(summed(adjoint(pull0_fed - pull1_fed)))

    early = covariance(side_by_side(start, obs_push))
    cov_start = summed_own(early[:, :width])
    cov_push = summed(early[:, width:])
    push_feed, push_state = mixtures(
        cov_push, [(down @ earlier @ later, first, ()), (earlier @ later, (), ())]
    )
    rhs_feed, rhs_state = mixtures(rhs, [(down @ earlier, first, ()), (earlier, (), ())])
    fed = tangent(side_by_side(rhs_feed, push_feed))
    fed_rhs = summed_own(fed[:, :width])
    fed_push = summed_own(fed[:, width:])

    cov_pull = summed(covariance(pull0))
    pull_feed, pull_state = mixtures(
        cov_pull, [(down @ earlier @ later @ up, first, first), (earlier @ later @ up, (), first)]
    )
    fed_pull = summed_own(tangent(pull_feed))

    dir_mult = pull0_later - start
    dir_state = rhs_state - pull_state
    moved = fed_rhs - fed_pull
    moved_turn = fed_pull + fed_push
    moved_whole = joined(moved)
    turn_mult = plus(pull0_later, push_later)
    if pull1 is not None:
        turn_mult = turn_mult - pull1_later
        cov_pull1 = summed(covariance(pull1))
        pull1_feed, pull1_state = mixtures(
            cov_pull1, [(down @ earlier @ later @ up, first, first), (earlier @ later @ up, (), first)]
        )
        pull_state = pull_state - pull1_state
        moved_turn = moved_turn - summed_own(tangent(pull1_feed))
    moved_feed, moved_state = mixtures(moved_whole, [(down @ earlier, first, first), (earlier, (), first)])
    if moved_feed is not None:
        moved_turn = moved_turn + summed_own(tangent(moved_feed))
    turn_state = moved_state + pull_state + push_state

    own_start = own(start)
    own_push = own(obs_push)
    own_pull = own(pull0)
    res1 = own(rhs) - cov_start
    image1 = res1 - moved
    turn1 = image1 - moved + moved_turn
    seen = observe(dir_state)
    own_data = lax.dynamic_slice_in_dim(data, group_index * rows, rows, 1)
    own_seen = lax.dynamic_slice_in_dim(seen, group_index * rows, rows, 1)
    image2 = own_data + own_seen
    turn2 = image2 + own_seen - observe(own(turn_state))
    (from_next,) = mixtures(own_start, [(up, (), ())])
    (pull_next,) = mixtures(own_pull, [(up, (), first)])
    (pull2_next,) = mixtures(pull2, [(up, (), first)])
    res3 = from_next - own_start + pull_next
    image3 = res3 + pull_next + own_push
    turn3 = image3 + pull_next - pull2_next + own_push + spread(own_seen / variance)
    if pull1 is not None:
        (pull1_next,) = mixtures(own(pull1), [(up, (), first)])
        image3 = image3 - pull1_next
        turn3 = turn3 - 2.0 * pull1_next

    def dot(left, right):
        return sum(jnp.sum(a * b) for a, b in zip(left, right))

    res = (res1, own_data, res3)
    image = (image1, image2, image3)
    turn = (turn1, turn2, turn3)
    sums = jnp.stack(
        [dot(image, res), dot(image, image), dot(turn, res), dot(turn, image), dot(turn, turn)]
    )
    sums = jnp.zeros((8, 128), jnp.float32).at[0, :5].set(sums)
    for axis in ("col", "grp", "sub"):
        size = lax.axis_size(axis)
        step = 1
        while step < size:
            sums = sums + lax.ppermute(sums, axis, [(i, i ^ step) for i in range(size)])
            step *= 2
    upper, square, turn_res, turn_image, turn_square = (sums[0, i] for i in range(5))
    alpha = upper / square
    alpha_next = (upper - alpha * square - alpha * (turn_res - alpha * turn_image)) / (
        square - 2.0 * alpha * turn_image + alpha * alpha * turn_square
    )
    keep = alpha + alpha_next * (1.0 - alpha)
    mixed = alpha * alpha_next
    multiplier = start + keep * dir_mult - mixed * turn_mult
    obs_multiplier = (alpha + alpha_next) * dir_obs - mixed * ((data + seen) / variance)
    increment = keep * dir_state + mixed * turn_state
    return (multiplier[None], obs_multiplier[None], increment[None])


def solution(mesh):
    placed = (
        P("sub", None, "col"),
        P("sub", "col", None),
        P("sub", None, "col"),
        P("sub", None, "col"),
        P("grp", None),
        P(None, "grp"),
        P("grp", None),
        P(),
        P(),
        P("sub", "col"),
        P("sub", "col"),
        P("sub", "col"),
    )
    return jax.shard_map(
        on_device,
        mesh=mesh,
        in_specs=placed,
        out_specs=(P("sub", None, "col"), P("sub", "col", None), P("sub", None, "col")),
        check_vma=False,
    )
```

```python
import math

import jax
import jax.numpy as jnp
import numpy as np
from jax import lax
from jax.experimental import pallas as pl
from jax.experimental.pallas import tpu as pltpu
from jax.sharding import PartitionSpec as P

KW = 128


F32 = jnp.float32
BF16 = jnp.bfloat16


def spectrum(scales, limits, total, count):
    waves = jnp.arange(count, dtype=jnp.int32)
    wavef = waves.astype(jnp.float32)
    decay = jnp.exp(-0.5 * (2.0 * math.pi * wavef[None, :] * scales[:, None] / total) ** 2)
    factor = jnp.where(waves == 0, 1.0, 2.0).astype(jnp.float32) / total
    keep = (waves[None, :] < limits[:, None]).astype(jnp.float32)
    values = decay * factor[None, :] * keep
    return jnp.concatenate([values, values], axis=1)


def spectral_table(count, coarse, fine):
    total = coarse * fine

    def small(columns):
        phase = columns[:, None] * jnp.arange(count, dtype=jnp.int32)[None, :] % total
        angle = 2.0 * math.pi / total * phase.astype(F32)
        return jnp.cos(angle), jnp.sin(angle)

    cos_a, sin_a = (t[:, None, :] for t in small(jnp.arange(coarse, dtype=jnp.int32) * fine))
    cos_b, sin_b = (t[None, :, :] for t in small(jnp.arange(fine, dtype=jnp.int32)))
    table = jnp.concatenate([cos_a * cos_b - sin_a * sin_b, sin_a * cos_b + cos_a * sin_b], axis=2)
    return table.reshape(total, 2 * count)


def rotated(block, axis, distance):
    size = lax.axis_size(axis)
    return lax.ppermute(block, axis, [(i, (i + distance) % size) for i in range(size)])


def mixtures(field, plans):
    size = lax.axis_size("sub")
    here = lax.axis_index("sub")
    masked = []
    for matrix, unread, zero in plans:
        weights = np.array(matrix, dtype=np.float32)
        live = np.ones_like(weights, dtype=bool)
        live[list(unread), :] = False
        live[:, list(zero)] = False
        masked.append((weights, live))
    arrived = {0: field}
    cells = {0: [(i, i) for i in range(size)]}
    for distance in range(1, size):
        steps = [((source + distance) % size, source) for source in range(size)]
        cells[distance] = [c for c in steps if any(w[c] * l[c] for w, l in masked)]
        if cells[distance]:
            arrived[distance] = lax.ppermute(field, "sub", [(source, dest) for dest, source in cells[distance]])
    results = []
    for weights, live in masked:
        total = None
        for distance, block in arrived.items():
            used = {float(weights[c]) for c in cells[distance] if live[c]}
            if not used or used == {0.0}:
                continue
            if len(used) > 1:
                factors = np.zeros(size, np.float32)
                for dest, source in cells[distance]:
                    factors[dest] = weights[dest, source]
                block = block * jnp.asarray(factors)[here]
            elif used != {1.0}:
                block = block * used.pop()
            total = block if total is None else total + block
        results.append(total)
    return results


def plus(*terms):
    kept = [term for term in terms if term is not None]
    return sum(kept[1:], kept[0]) if kept else None


def halves(value):
    high = value.astype(BF16)
    return high, (value - high.astype(F32)).astype(BF16)


def contract(left, right, over):
    return lax.dot_general(left, right, (((over[0],), (over[1],)), ((), ())), preferred_element_type=F32)


def contract3(left, right, over):
    left_high, left_low = left
    right_high, right_low = right
    return (
        contract(left_high, right_low, over)
        + contract(left_low, right_high, over)
        + contract(left_high, right_high, over)
    )


def mixed_rows(left, right, fine, over):
    high, low = left
    right_high, right_low = right
    if high.shape[0] == fine:
        return contract3(left, right, over)
    wide = contract(jnp.concatenate([high, low], axis=0), right_high, over)
    exact = wide[:fine] + wide[high.shape[0] :] + contract(high[:fine], right_low, over)
    return jnp.concatenate([exact, wide[fine : high.shape[0]]], axis=0)


def fine_low(value, fine):
    high = value.astype(BF16)
    return high, (value[:fine] - high[:fine].astype(F32)).astype(BF16)


def call(kernel, out, inputs, flops, grid=None, in_specs=None, out_specs=None, scratch=()):
    vmem = pl.BlockSpec(memory_space=pltpu.VMEM)
    smem = pl.BlockSpec(memory_space=pltpu.SMEM)
    if in_specs is None:
        in_specs = [smem if jnp.issubdtype(x.dtype, jnp.integer) else vmem for x in inputs]
        out_specs = jax.tree.map(lambda _: vmem, out)
    size = sum(math.prod(x.shape) * x.dtype.itemsize for x in [*inputs, *jax.tree.leaves(out)])
    return pl.pallas_call(
        kernel,
        out_shape=out,
        grid=grid or (),
        in_specs=in_specs,
        out_specs=out_specs,
        scratch_shapes=scratch,
        cost_estimate=pl.CostEstimate(flops=flops, bytes_accessed=size, transcendentals=0),
        compiler_params=pltpu.CompilerParams(vmem_limit_bytes=40 * 1024 * 1024),
    )(*inputs)


def shape(*dims):
    return jax.ShapeDtypeStruct(dims, F32)


def on_device(
    first_rhs,
    innovations,
    start_mult,
    trajectory,
    weight_in,
    weight_out,
    vertical_modes,
    length_scale,
    band_limit,
    obs_col,
    obs_count,
    obs_var,
):
    data = innovations[0]
    variance = obs_var[0][:, None]
    depth, width = first_rhs.shape[1:]
    slots = data.shape[0]
    subs = lax.axis_size("sub")
    shards = lax.axis_size("col")
    groups = lax.axis_size("grp")
    here = lax.axis_index("sub")
    column_index = lax.axis_index("col")
    group_index = lax.axis_index("grp")
    total_cols = width * shards
    hidden = weight_in.shape[0]
    half_modes = vertical_modes.shape[0]
    owned_modes = half_modes // shards
    rows = width // groups
    steps = 4
    block = hidden // steps

    ones = np.ones((subs, subs))
    up = np.eye(subs, k=1)
    down = np.eye(subs, k=-1)
    later = np.triu(ones)
    earlier = np.tril(ones)
    first = (0,)
    place = jnp.stack([group_index, here]).astype(jnp.int32)

    def turned(place_ref, ref, value):
        for step in range(groups):
            ref[step] = value_rows(value, lax.rem(place_ref[0] + step, groups))

    def value_rows(value, index):
        total = value[:rows]
        for other in range(1, groups):
            total = jnp.where(index == other, value[other * rows : (other + 1) * rows], total)
        return total

    def own_rows(place_ref, ref):
        return ref[pl.ds(pl.multiple_of(place_ref[0] * rows, rows), rows), :]

    def own(field):
        return lax.dynamic_slice_in_dim(field, group_index * rows, rows, 0)

    def sent(partial):
        return [rotated(partial, "grp", step) for step in range(1, groups)]

    def sent_parts(parts):
        return [parts[0], *(rotated(parts[step], "grp", step) for step in range(1, groups))]

    def summed_own(parts):
        return plus(*sent_parts(parts))

    def summed(partial):
        return plus(partial, *sent(partial))

    def joined(part):
        whole = lax.dynamic_update_slice_in_dim(jnp.zeros((width, depth), F32), part, group_index * rows, 0)
        for step in range(1, groups):
            source = (group_index - step) % groups
            whole = lax.dynamic_update_slice_in_dim(whole, rotated(part, "grp", step), source * rows, 0)
        return whole

    before = lax.ppermute(trajectory[0].astype(F32), "sub", [(i, i + 1) for i in range(subs - 1)])

    local_cols = obs_col[0] - column_index * width
    live = (jnp.arange(slots, dtype=jnp.int32) < obs_count[0, 0]).astype(F32)
    pick = (jnp.arange(width, dtype=jnp.int32)[:, None] == local_cols[None, :]).astype(F32)
    mine = ((local_cols // rows) == group_index).astype(F32)[:, None]
    pick = pick * live[None, :]

    def picked(values, chosen):
        high, low = halves(values)
        chosen = chosen.astype(BF16)
        return contract(chosen, high, (1, 0)) + contract(chosen, low, (1, 0))

    def seen_by(chosen, field):
        high, low = halves(field)
        chosen = chosen.astype(BF16)
        return contract(chosen, high, (0, 0)) + contract(chosen, low, (0, 0))

    def opening(start_ref, rhs_ref, data_ref, variance_ref, pick_ref, modes_ref, start_out, push_out, rhs_out, amp_ref):
        start_t = start_ref[...].T
        push_t = picked(data_ref[...] / variance_ref[...], pick_ref[...])
        start_out[...] = start_t
        push_out[...] = push_t
        rhs_out[...] = rhs_ref[...].T
        modes = halves(modes_ref[...])
        amp_ref[:, :width] = contract(modes[0], start_t.astype(BF16), (1, 1))
        amp_ref[:, width:] = contract3(modes, halves(push_t), (1, 1))

    start, push, rhs, amp_early = call(
        opening,
        [shape(width, depth)] * 3 + [shape(half_modes, 2 * width)],
        [start_mult[0], first_rhs[0], data, variance, pick, vertical_modes],
        8 * half_modes * depth * width,
    )
    whole_spec = [pl.BlockSpec(memory_space=pltpu.SMEM)]

    def fixed(*dims):
        return pl.BlockSpec(dims, lambda i: (0,) * len(dims))

    in_block = pl.BlockSpec((block, depth), lambda i: (i, 0))
    out_block = pl.BlockSpec((depth, block), lambda i: (0, i))
    slope_block = pl.BlockSpec((width, block), lambda i: (0, i))

    def slopes_and_adjoint(place_ref, fine_ref, rough_ref, before_ref, win_ref, wout_ref, fine_out, rough_out, slopes_ref, total_ref, turned_ref):
        index = pl.program_id(0)

        @pl.when(index == 0)
        def _():
            total_ref[...] = jnp.zeros_like(total_ref)
            turned_ref[...] = before_ref[...].T.astype(BF16)

        win = halves(win_ref[...])
        wout = halves(wout_ref[...])
        state = turned_ref[...]
        bend = jnp.tanh(contract(state, win[1], (1, 1)) + contract(state, win[0], (1, 1)))
        slopes = (1.0 - bend * bend) * (place_ref[1] > 0).astype(F32)
        slopes_ref[...] = slopes
        fields = fine_low(jnp.concatenate([fine_ref[...], rough_ref[...]], axis=0), width)
        inner = mixed_rows(fields, wout, width, (1, 0)) * jnp.concatenate([slopes, slopes], axis=0)
        total_ref[...] += mixed_rows(fine_low(inner, width), win, width, (1, 0))

        @pl.when(index == steps - 1)
        def _():
            fine_out[...] = total_ref[:width]
            turned(place_ref, rough_out, total_ref[width:])

    push_fed, push_later = mixtures(push, [(later, first, ()), (later, (), ())])
    pull0_part, pull2_parts, slopes = call(
        slopes_and_adjoint,
        [shape(width, depth), shape(groups, rows, depth), shape(width, hidden)],
        [place, start, push_fed, before, weight_in, weight_out],
        20 * hidden * depth * width,
        grid=(steps,),
        in_specs=whole_spec + [fixed(width, depth)] * 2 + [fixed(depth, width), in_block, out_block],
        out_specs=[fixed(width, depth), fixed(groups, rows, depth), slope_block],
        scratch=[pltpu.VMEM((2 * width, depth), F32), pltpu.VMEM((width, depth), BF16)],
    )

    def adjoint(field):
        def kernel(field_ref, slopes_ref, win_ref, wout_ref, total_ref):
            @pl.when(pl.program_id(0) == 0)
            def _():
                total_ref[...] = jnp.zeros_like(total_ref)

            inner = contract3(halves(field_ref[...]), halves(wout_ref[...]), (1, 0)) * slopes_ref[...]
            total_ref[...] += contract3(halves(inner), halves(win_ref[...]), (1, 0))

        return call(
            kernel,
            shape(width, depth),
            [field, slopes, weight_in, weight_out],
            12 * hidden * depth * width,
            grid=(steps,),
            in_specs=[fixed(width, depth), slope_block, in_block, out_block],
            out_specs=fixed(width, depth),
        )

    def tangent(fine, rough=None):
        count = 1 if rough is None else 2

        def kernel(place_ref, *refs):
            fields, (slopes_ref, win_ref, wout_ref), outs, total_ref = (
                refs[:count],
                refs[count : count + 3],
                refs[count + 3 : -1],
                refs[-1],
            )

            @pl.when(pl.program_id(0) == 0)
            def _():
                total_ref[...] = jnp.zeros_like(total_ref)

            both = fine_low(jnp.concatenate([r[...] for r in fields], axis=0), width)
            slope = slopes_ref[...]
            inner = mixed_rows(both, halves(win_ref[...]), width, (1, 1)) * jnp.concatenate([slope] * count, axis=0)
            total_ref[...] += mixed_rows(fine_low(inner, width), halves(wout_ref[...]), width, (1, 1))

            @pl.when(pl.program_id(0) == steps - 1)
            def _():
                for i, out in enumerate(outs):
                    turned(place_ref, out, total_ref[i * width : (i + 1) * width])

        return call(
            kernel,
            [shape(groups, rows, depth)] * count,
            [place, fine, *([] if rough is None else [rough]), slopes, weight_in, weight_out],
            (12 if rough is None else 16) * hidden * depth * width,
            grid=(steps,),
            in_specs=whole_spec + [fixed(width, depth)] * count + [slope_block, in_block, out_block],
            out_specs=[fixed(groups, rows, depth)] * count,
            scratch=[pltpu.VMEM((count * width, depth), F32)],
        )

    seed, pull0_part = lax.optimization_barrier((jnp.zeros((), jnp.int32), pull0_part))
    first_mode = group_index * half_modes + column_index * owned_modes + seed
    owned_scales = lax.dynamic_slice_in_dim(length_scale, first_mode, owned_modes, 0)
    owned_limits = lax.dynamic_slice_in_dim(band_limit, first_mode, owned_modes, 0)
    owned_spec = spectrum(owned_scales, owned_limits, total_cols, KW)
    fine_cols = 1 << (total_cols.bit_length() // 2)
    table = spectral_table(KW, total_cols // fine_cols, fine_cols)

    def amplitudes(field_parts):
        def kernel(*refs):
            modes_ref, whole_ref, amp_ref = refs[-3:]
            whole = plus(*(r[...] for r in refs[:-3]))
            whole_ref[...] = whole
            amp_ref[...] = contract3(halves(modes_ref[...]), halves(whole), (1, 1))

        return call(
            kernel,
            [shape(width, depth), shape(half_modes, width)],
            [*field_parts, vertical_modes],
            6 * half_modes * depth * width,
        )

    def correlated(amp):
        count = amp.shape[1] // width
        owned = lax.all_to_all(amp.reshape(shards, owned_modes, count * width), "col", 0, 0, tiled=True)

        def kernel(owned_ref, table_ref, spec_ref, back_ref):
            parts = halves(table_ref[...])
            for i in range(count):
                lanes = slice(i * width, (i + 1) * width)
                modes = jnp.concatenate([owned_ref[c][:, lanes] for c in range(shards)], axis=1)
                coeffs = contract3(halves(modes), parts, (1, 0)) * spec_ref[...]
                back = contract3(halves(coeffs), parts, (1, 1))
                for c in range(shards):
                    back_ref[c, :, lanes] = back[:, c * width : (c + 1) * width]

        back = call(
            kernel,
            shape(*owned.shape),
            [owned, table, owned_spec],
            12 * owned_modes * count * total_cols * 2 * KW,
        )
        returned = lax.all_to_all(back, "col", 0, 0, tiled=True)
        return returned.reshape(half_modes, count * width)

    def back_to_columns(returned):
        def kernel(returned_ref, modes_ref, out_ref):
            out_ref[...] = contract3(halves(returned_ref[...].T), halves(modes_ref[...]), (1, 0))

        return call(
            kernel, shape(width, depth), [returned, vertical_modes], 6 * half_modes * depth * width
        )

    def back_to_columns_early(returned):
        def kernel(place_ref, returned_ref, modes_ref, rough_out, fine_out):
            modes = halves(modes_ref[...])
            back = returned_ref[...].T
            turned(place_ref, rough_out, contract(back[:width].astype(BF16), modes[0], (1, 0)))
            fine_out[...] = contract3(halves(back[width:]), modes, (1, 0))

        return call(
            kernel,
            [shape(groups, rows, depth), shape(width, depth)],
            [place, returned, vertical_modes],
            8 * half_modes * depth * width,
        )

    def covariance_sum(field):
        return summed(back_to_columns(correlated(amplitudes([field])[1])))

    pull0, amp_pull = amplitudes([pull0_part, *sent(pull0_part)])
    cov_start_parts, cov_push_part = back_to_columns_early(correlated(amp_early))
    cov_push = summed(cov_push_part)
    push_feed, push_state = mixtures(
        cov_push, [(down @ earlier @ later, first, ()), (earlier @ later, (), ())]
    )
    rhs_feed, rhs_state = mixtures(rhs, [(down @ earlier, first, ()), (earlier, (), ())])
    fed_rhs_parts, fed_push_parts = tangent(rhs_feed, push_feed)
    fed_rhs = summed_own(fed_rhs_parts)
    fed_push = summed_own(fed_push_parts)
    cov_start = summed_own(cov_start_parts)
    pull2 = summed_own(pull2_parts)

    cov_pull = summed(back_to_columns(correlated(amp_pull)))
    pull_feed, pull_state = mixtures(
        cov_pull, [(down @ earlier @ later @ up, first, first), (earlier @ later @ up, (), first)]
    )
    fed_pull = summed_own(tangent(pull_feed)[0])
    pull0_fed, pull0_later = mixtures(pull0, [(later @ up, first, first), (later @ up, (), first)])

    moved = fed_rhs - fed_pull
    moved_turn = fed_pull + fed_push
    turn_mult = plus(pull0_later, push_later)
    pull1 = None
    if pull0_fed is not None:
        pull1 = summed(adjoint(pull0_fed))
        pull1_fed, pull1_later = mixtures(pull1, [(later @ up, first, first), (later @ up, (), first)])
        pull2 = pull2 + own(summed(adjoint(pull0_fed - pull1_fed)))
        turn_mult = turn_mult - pull1_later
        cov_pull1 = covariance_sum(pull1)
        pull1_feed, pull1_state = mixtures(
            cov_pull1, [(down @ earlier @ later @ up, first, first), (earlier @ later @ up, (), first)]
        )
        push_state = push_state - pull1_state
        moved_turn = moved_turn - summed_own(tangent(pull1_feed)[0])
    moved_feed, moved_state = mixtures(moved, [(down @ earlier, first, first), (earlier, (), first)])
    if moved_feed is not None:
        moved_turn = moved_turn + summed_own(tangent(joined(moved_feed))[0])

    (start_next,) = mixtures(own(start), [(up, (), ())])
    pull_shift = 2.0 * own(pull0)
    pull_step = own(pull0) - pull2
    if pull1 is not None:
        own_pull1 = own(pull1)
        pull_shift = pull_shift - own_pull1
        pull_step = pull_step - own_pull1
        (pull_next,) = mixtures(own(pull0), [(up, (), first)])
    (shift_next,) = mixtures(pull_shift, [(up, (), first)])
    (step_next,) = mixtures(pull_step, [(up, (), first)])
    if pull1 is None:
        pull_next = 0.5 * shift_next

    def inner_products(
        place_ref, rhs_ref, cov_start_ref, moved_ref, moved_turn_ref, moved_state_ref, data_ref, variance_ref,
        pick_ref, mine_ref, rhs_state_ref, pull_state_ref, push_state_ref, start_ref, push_ref,
        start_next_ref, pull_next_ref, shift_next_ref, step_next_ref, sums_ref,
    ):
        moved = moved_ref[...]
        pull_own = own_rows(place_ref, pull_state_ref)
        state = own_rows(place_ref, rhs_state_ref) - pull_own
        turn_state = moved_state_ref[...] + pull_own + own_rows(place_ref, push_state_ref)
        res1 = own_rows(place_ref, rhs_ref) - cov_start_ref[...]
        image1 = res1 - moved
        turn1 = image1 - moved + moved_turn_ref[...]
        mine = mine_ref[...]
        chosen = own_rows(place_ref, pick_ref)
        res2 = data_ref[...] * mine
        seen = seen_by(chosen, state)
        image2 = res2 + seen
        turn2 = image2 + seen - seen_by(chosen, turn_state)
        push = own_rows(place_ref, push_ref)
        from_next = start_next_ref[...] - own_rows(place_ref, start_ref)
        res3 = from_next + pull_next_ref[...]
        image3 = from_next + shift_next_ref[...] + push
        turn3 = image3 + step_next_ref[...] + push + picked(seen / variance_ref[...], chosen)
        res = (res1, res2, res3)
        image = (image1, image2, image3)
        turn = (turn1, turn2, turn3)
        lane = lax.broadcasted_iota(jnp.int32, sums_ref.shape, 1)
        sums = jnp.zeros(sums_ref.shape, F32)
        for i, (left, right) in enumerate(((image, res), (image, image), (turn, res), (turn, image), (turn, turn))):
            value = sum(jnp.sum(a * b) for a, b in zip(left, right))
            sums = jnp.where(lane == i, value, sums)
        sums_ref[...] = sums

    everyone = ("sub", "col", "grp")
    devices = subs * shards * groups
    sums = call(
        inner_products,
        shape(devices, 128),
        [
            place, rhs, cov_start, moved, moved_turn, moved_state, data, variance, pick, mine,
            rhs_state, pull_state, push_state, start, push, start_next, pull_next, shift_next, step_next,
        ],
        1000000,
    )
    sums = lax.all_to_all(sums, everyone, 0, 0, tiled=True)
    moved_state = joined(moved_state)

    def closing(
        sums_ref, start_ref, pull_later_ref, turn_mult_ref, data_ref, variance_ref, pick_ref,
        rhs_state_ref, pull_state_ref, push_state_ref, moved_state_ref, mult_ref, obs_ref, inc_ref,
    ):
        totals = jnp.sum(sums_ref[...], axis=0, keepdims=True)
        upper, square, turn_res, turn_image, turn_square = (totals[:, i : i + 1] for i in range(5))
        alpha = upper / square
        alpha_next = (upper - alpha * square - alpha * (turn_res - alpha * turn_image)) / (
            square - 2.0 * alpha * turn_image + alpha * alpha * turn_square
        )
        keep = alpha + alpha_next * (1.0 - alpha)
        mixed = alpha * alpha_next
        start_t = start_ref[...]
        state = rhs_state_ref[...] - pull_state_ref[...]
        turn_state = moved_state_ref[...] + pull_state_ref[...] + push_state_ref[...]
        mult_ref[...] = (start_t + keep * (pull_later_ref[...] - start_t) - mixed * turn_mult_ref[...]).T
        inc_ref[...] = (keep * state + mixed * turn_state).T
        seen = seen_by(pick_ref[...], state)
        data_t = data_ref[...]
        obs_ref[...] = ((alpha + alpha_next) * data_t - mixed * (data_t + seen)) / variance_ref[...]

    multiplier, obs_multiplier, increment = call(
        closing,
        [shape(depth, width), shape(slots, depth), shape(depth, width)],
        [
            sums, start, pull0_later, turn_mult, data, variance, pick,
            rhs_state, pull_state, push_state, moved_state,
        ],
        1000000,
    )
    return (multiplier[None], obs_multiplier[None], increment[None])


def solution(mesh):
    placed = (
        P("sub", None, "col"),
        P("sub", "col", None),
        P("sub", None, "col"),
        P("sub", None, "col"),
        P("grp", None),
        P(None, "grp"),
        P("grp", None),
        P(),
        P(),
        P("sub", "col"),
        P("sub", "col"),
        P("sub", "col"),
    )
    return jax.shard_map(
        on_device,
        mesh=mesh,
        in_specs=placed,
        out_specs=(P("sub", None, "col"), P("sub", "col", None), P("sub", None, "col")),
        check_vma=False,
    )
```

```python
import math

import jax
import jax.numpy as jnp
import numpy as np
from jax import lax
from jax.experimental import pallas as pl
from jax.experimental.pallas import tpu as pltpu
from jax.sharding import PartitionSpec as P

KW = 128


F32 = jnp.float32
BF16 = jnp.bfloat16


def spectrum(scales, limits, total, count):
    waves = jnp.arange(count, dtype=jnp.int32)
    wavef = waves.astype(jnp.float32)
    decay = jnp.exp(-0.5 * (2.0 * math.pi * wavef[None, :] * scales[:, None] / total) ** 2)
    factor = jnp.where(waves == 0, 1.0, 2.0).astype(jnp.float32) / total
    keep = (waves[None, :] < limits[:, None]).astype(jnp.float32)
    values = decay * factor[None, :] * keep
    return jnp.concatenate([values, values], axis=1)


def spectral_table(count, coarse, fine, origin):
    total = coarse * fine

    def small(columns):
        phase = (columns[:, None] + origin) * jnp.arange(count, dtype=jnp.int32)[None, :] % total
        angle = 2.0 * math.pi / total * phase.astype(F32)
        return jnp.cos(angle), jnp.sin(angle)

    cos_a, sin_a = (t[:, None, :] for t in small(jnp.arange(coarse, dtype=jnp.int32) * fine))
    cos_b, sin_b = (t[None, :, :] for t in small(jnp.arange(fine, dtype=jnp.int32)))
    table = jnp.concatenate([cos_a * cos_b - sin_a * sin_b, sin_a * cos_b + cos_a * sin_b], axis=2)
    return table.reshape(total, 2 * count)


def rotated(block, axis, distance):
    size = lax.axis_size(axis)
    return lax.ppermute(block, axis, [(i, (i + distance) % size) for i in range(size)])


def mixtures(field, plans):
    size = lax.axis_size("sub")
    here = lax.axis_index("sub")
    masked = []
    for matrix, unread, zero in plans:
        weights = np.array(matrix, dtype=np.float32)
        live = np.ones_like(weights, dtype=bool)
        live[list(unread), :] = False
        live[:, list(zero)] = False
        masked.append((weights, live))
    arrived = {0: field}
    cells = {0: [(i, i) for i in range(size)]}
    for distance in range(1, size):
        steps = [((source + distance) % size, source) for source in range(size)]
        cells[distance] = [c for c in steps if any(w[c] * l[c] for w, l in masked)]
        if cells[distance]:
            arrived[distance] = lax.ppermute(field, "sub", [(source, dest) for dest, source in cells[distance]])
    results = []
    for weights, live in masked:
        total = None
        for distance, block in arrived.items():
            used = {float(weights[c]) for c in cells[distance] if live[c]}
            if not used or used == {0.0}:
                continue
            if len(used) > 1:
                factors = np.zeros(size, np.float32)
                for dest, source in cells[distance]:
                    factors[dest] = weights[dest, source]
                block = block * jnp.asarray(factors)[here]
            elif used != {1.0}:
                block = block * used.pop()
            total = block if total is None else total + block
        results.append(total)
    return results


def plus(*terms):
    kept = [term for term in terms if term is not None]
    return sum(kept[1:], kept[0]) if kept else None


def halves(value):
    high = value.astype(BF16)
    return high, (value - high.astype(F32)).astype(BF16)


def contract(left, right, over):
    return lax.dot_general(left, right, (((over[0],), (over[1],)), ((), ())), preferred_element_type=F32)


def contract3(left, right, over):
    left_high, left_low = left
    right_high, right_low = right
    return (
        contract(left_high, right_low, over)
        + contract(left_low, right_high, over)
        + contract(left_high, right_high, over)
    )


def mixed_rows(left, right, fine, over):
    high, low = left
    right_high, right_low = right
    if high.shape[0] == fine:
        return contract3(left, right, over)
    wide = contract(jnp.concatenate([high, low], axis=0), right_high, over)
    exact = wide[:fine] + wide[high.shape[0] :] + contract(high[:fine], right_low, over)
    return jnp.concatenate([exact, wide[fine : high.shape[0]]], axis=0)


def fine_low(value, fine):
    high = value.astype(BF16)
    return high, (value[:fine] - high[:fine].astype(F32)).astype(BF16)


def call(kernel, out, inputs, flops, vmem_mib=16, grid=None, in_specs=None, out_specs=None, scratch=()):
    vmem = pl.BlockSpec(memory_space=pltpu.VMEM)
    smem = pl.BlockSpec(memory_space=pltpu.SMEM)
    if in_specs is None:
        in_specs = [smem if jnp.issubdtype(x.dtype, jnp.integer) else vmem for x in inputs]
        out_specs = jax.tree.map(lambda _: vmem, out)
    size = sum(math.prod(x.shape) * x.dtype.itemsize for x in [*inputs, *jax.tree.leaves(out)])
    return pl.pallas_call(
        kernel,
        out_shape=out,
        grid=grid or (),
        in_specs=in_specs,
        out_specs=out_specs,
        scratch_shapes=scratch,
        cost_estimate=pl.CostEstimate(flops=flops, bytes_accessed=size, transcendentals=0),
        compiler_params=pltpu.CompilerParams(vmem_limit_bytes=vmem_mib * 1024 * 1024),
    )(*inputs)


def shape(*dims):
    return jax.ShapeDtypeStruct(dims, F32)


def on_device(
    first_rhs,
    innovations,
    start_mult,
    trajectory,
    weight_in,
    weight_out,
    vertical_modes,
    length_scale,
    band_limit,
    obs_col,
    obs_count,
    obs_var,
):
    data = innovations[0]
    variance = obs_var[0][:, None]
    depth, width = first_rhs.shape[1:]
    slots = data.shape[0]
    subs = lax.axis_size("sub")
    shards = lax.axis_size("col")
    groups = lax.axis_size("grp")
    here = lax.axis_index("sub")
    column_index = lax.axis_index("col")
    group_index = lax.axis_index("grp")
    total_cols = width * shards
    hidden = weight_in.shape[0]
    half_modes = vertical_modes.shape[0]
    owned_modes = half_modes // shards
    rows = width // groups
    steps = 4
    block = hidden // steps

    ones = np.ones((subs, subs))
    up = np.eye(subs, k=1)
    down = np.eye(subs, k=-1)
    later = np.triu(ones)
    earlier = np.tril(ones)
    first = (0,)
    place = jnp.stack([group_index, here]).astype(jnp.int32)

    def turned(place_ref, ref, value):
        for step in range(groups):
            ref[step] = value_rows(value, lax.rem(place_ref[0] + step, groups))

    def value_rows(value, index):
        total = value[:rows]
        for other in range(1, groups):
            total = jnp.where(index == other, value[other * rows : (other + 1) * rows], total)
        return total

    def own_rows(place_ref, ref):
        return ref[pl.ds(pl.multiple_of(place_ref[0] * rows, rows), rows), :]

    def own(field):
        return lax.dynamic_slice_in_dim(field, group_index * rows, rows, 0)

    def sent(partial):
        return [rotated(partial, "grp", step) for step in range(1, groups)]

    def summed_own(parts):
        return plus(parts[0], *(rotated(parts[step], "grp", step) for step in range(1, groups)))

    def summed(partial):
        return plus(partial, *sent(partial))

    def joined(part):
        whole = lax.dynamic_update_slice_in_dim(jnp.zeros((width, depth), F32), part, group_index * rows, 0)
        for step in range(1, groups):
            source = (group_index - step) % groups
            whole = lax.dynamic_update_slice_in_dim(whole, rotated(part, "grp", step), source * rows, 0)
        return whole

    before = lax.ppermute(trajectory[0].astype(F32), "sub", [(i, i + 1) for i in range(subs - 1)])

    local_cols = obs_col[0] - column_index * width
    live = (jnp.arange(slots, dtype=jnp.int32) < obs_count[0, 0]).astype(F32)
    pick = (jnp.arange(width, dtype=jnp.int32)[:, None] == local_cols[None, :]).astype(F32)
    mine = ((local_cols // rows) == group_index).astype(F32)[:, None]
    pick = pick * live[None, :]

    def picked(values, chosen):
        high, low = halves(values)
        chosen = chosen.astype(BF16)
        return contract(chosen, high, (1, 0)) + contract(chosen, low, (1, 0))

    def seen_by(chosen, field):
        high, low = halves(field)
        chosen = chosen.astype(BF16)
        return contract(chosen, high, (0, 0)) + contract(chosen, low, (0, 0))

    def opening(start_ref, rhs_ref, data_ref, variance_ref, pick_ref, modes_ref, start_out, push_out, rhs_out, amp_ref):
        start_t = start_ref[...].T
        push_t = picked(data_ref[...] / variance_ref[...], pick_ref[...])
        start_out[...] = start_t
        push_out[...] = push_t
        rhs_out[...] = rhs_ref[...].T
        modes = halves(modes_ref[...])
        amp_ref[:, :width] = contract(modes[0], start_t.astype(BF16), (1, 1))
        amp_ref[:, width:] = contract3(modes, halves(push_t), (1, 1))

    start, push, rhs, amp_early = call(
        opening,
        [shape(width, depth)] * 3 + [shape(half_modes, 2 * width)],
        [start_mult[0], first_rhs[0], data, variance, pick, vertical_modes],
        8 * half_modes * depth * width,
    )
    whole_spec = [pl.BlockSpec(memory_space=pltpu.SMEM)]

    def fixed(*dims):
        return pl.BlockSpec(dims, lambda i: (0,) * len(dims))

    in_block = pl.BlockSpec((block, depth), lambda i: (i, 0))
    out_block = pl.BlockSpec((depth, block), lambda i: (0, i))
    slope_block = pl.BlockSpec((width, block), lambda i: (0, i))

    def slopes_and_adjoint(place_ref, fine_ref, rough_ref, before_ref, win_ref, wout_ref, fine_out, rough_out, slopes_ref, total_ref, turned_ref):
        index = pl.program_id(0)

        @pl.when(index == 0)
        def _():
            total_ref[...] = jnp.zeros_like(total_ref)
            turned_ref[...] = before_ref[...].T.astype(BF16)

        win = halves(win_ref[...])
        wout = halves(wout_ref[...])
        state = turned_ref[...]
        bend = jnp.tanh(contract(state, win[1], (1, 1)) + contract(state, win[0], (1, 1)))
        slopes = (1.0 - bend * bend) * (place_ref[1] > 0).astype(F32)
        slopes_ref[...] = slopes
        fields = fine_low(jnp.concatenate([fine_ref[...], rough_ref[...]], axis=0), width)
        inner = mixed_rows(fields, wout, width, (1, 0)) * jnp.concatenate([slopes, slopes], axis=0)
        total_ref[...] += mixed_rows(fine_low(inner, width), win, width, (1, 0))

        @pl.when(index == steps - 1)
        def _():
            fine_out[...] = total_ref[:width]
            turned(place_ref, rough_out, total_ref[width:])

    push_fed, push_later = mixtures(push, [(later, first, ()), (later, (), ())])
    pull0_part, pull2_parts, slopes = call(
        slopes_and_adjoint,
        [shape(width, depth), shape(groups, rows, depth), shape(width, hidden)],
        [place, start, push_fed, before, weight_in, weight_out],
        20 * hidden * depth * width,
        vmem_mib=20,
        grid=(steps,),
        in_specs=whole_spec + [fixed(width, depth)] * 2 + [fixed(depth, width), in_block, out_block],
        out_specs=[fixed(width, depth), fixed(groups, rows, depth), slope_block],
        scratch=[pltpu.VMEM((2 * width, depth), F32), pltpu.VMEM((width, depth), BF16)],
    )

    def adjoint(field):
        def kernel(field_ref, slopes_ref, win_ref, wout_ref, total_ref):
            @pl.when(pl.program_id(0) == 0)
            def _():
                total_ref[...] = jnp.zeros_like(total_ref)

            inner = contract3(halves(field_ref[...]), halves(wout_ref[...]), (1, 0)) * slopes_ref[...]
            total_ref[...] += contract3(halves(inner), halves(win_ref[...]), (1, 0))

        return call(
            kernel,
            shape(width, depth),
            [field, slopes, weight_in, weight_out],
            12 * hidden * depth * width,
            vmem_mib=20,
            grid=(steps,),
            in_specs=[fixed(width, depth), slope_block, in_block, out_block],
            out_specs=fixed(width, depth),
        )

    def tangent(fine, rough=None):
        count = 1 if rough is None else 2

        def kernel(place_ref, *refs):
            fields, (slopes_ref, win_ref, wout_ref, out_ref, total_ref) = refs[:count], refs[count:]

            @pl.when(pl.program_id(0) == 0)
            def _():
                total_ref[...] = jnp.zeros_like(total_ref)

            both = fine_low(jnp.concatenate([r[...] for r in fields], axis=0), width)
            slope = slopes_ref[...]
            inner = mixed_rows(both, halves(win_ref[...]), width, (1, 1)) * jnp.concatenate([slope] * count, axis=0)
            total_ref[...] += mixed_rows(fine_low(inner, width), halves(wout_ref[...]), width, (1, 1))

            @pl.when(pl.program_id(0) == steps - 1)
            def _():
                for i in range(count):
                    turned(
                        place_ref,
                        out_ref.at[:, i * rows : (i + 1) * rows],
                        total_ref[i * width : (i + 1) * width],
                    )

        parts = call(
            kernel,
            shape(groups, count * rows, depth),
            [place, fine, *([] if rough is None else [rough]), slopes, weight_in, weight_out],
            (12 if rough is None else 16) * hidden * depth * width,
            vmem_mib=20,
            grid=(steps,),
            in_specs=whole_spec + [fixed(width, depth)] * count + [slope_block, in_block, out_block],
            out_specs=fixed(groups, count * rows, depth),
            scratch=[pltpu.VMEM((count * width, depth), F32)],
        )
        return summed_own(parts)

    seed, amp_early = lax.optimization_barrier((place[0], amp_early))
    seed = seed - group_index
    first_mode = group_index * half_modes + column_index * owned_modes + seed
    owned_scales = lax.dynamic_slice_in_dim(length_scale, first_mode, owned_modes, 0)
    owned_limits = lax.dynamic_slice_in_dim(band_limit, first_mode, owned_modes, 0)
    owned_spec = spectrum(owned_scales, owned_limits, total_cols, KW)
    fine_cols = 1 << (total_cols.bit_length() // 2)
    table = spectral_table(KW, total_cols // fine_cols, fine_cols, seed)

    def amplitudes(field_parts):
        def kernel(*refs):
            modes_ref, whole_ref, amp_ref = refs[-3:]
            whole = plus(*(r[...] for r in refs[:-3]))
            whole_ref[...] = whole
            amp_ref[...] = contract3(halves(modes_ref[...]), halves(whole), (1, 1))

        return call(
            kernel,
            [shape(width, depth), shape(half_modes, width)],
            [*field_parts, vertical_modes],
            6 * half_modes * depth * width,
        )

    def correlated(amp):
        count = amp.shape[1] // width
        owned = lax.all_to_all(amp.reshape(shards, owned_modes, count * width), "col", 0, 0, tiled=True)

        def kernel(owned_ref, table_ref, spec_ref, back_ref):
            parts = halves(table_ref[...])
            for i in range(count):
                lanes = slice(i * width, (i + 1) * width)
                modes = jnp.concatenate([owned_ref[c][:, lanes] for c in range(shards)], axis=1)
                coeffs = contract3(halves(modes), parts, (1, 0)) * spec_ref[...]
                back = contract3(halves(coeffs), parts, (1, 1))
                for c in range(shards):
                    back_ref[c, :, lanes] = back[:, c * width : (c + 1) * width]

        back = call(
            kernel, shape(*owned.shape), [owned, table, owned_spec], 12 * owned_modes * count * total_cols * 2 * KW
        )
        returned = lax.all_to_all(back, "col", 0, 0, tiled=True)
        return returned.reshape(half_modes, count * width)

    def back_to_columns(returned):
        def kernel(returned_ref, modes_ref, out_ref):
            out_ref[...] = contract3(halves(returned_ref[...].T), halves(modes_ref[...]), (1, 0))

        return call(kernel, shape(width, depth), [returned, vertical_modes], 6 * half_modes * depth * width)

    def back_to_columns_early(returned, beside):
        def kernel(place_ref, returned_ref, modes_ref, beside_ref, rough_out, fine_out):
            modes = halves(modes_ref[...])
            back = returned_ref[...].T
            turned(place_ref, rough_out.at[:, :rows], contract(back[:width].astype(BF16), modes[0], (1, 0)))
            rough_out[:, rows:] = beside_ref[...]
            fine_out[...] = contract3(halves(back[width:]), modes, (1, 0))

        return call(
            kernel,
            [shape(groups, 2 * rows, depth), shape(width, depth)],
            [place, returned, vertical_modes, beside],
            8 * half_modes * depth * width,
        )

    def covariance_sum(field):
        amp = amplitudes([field])[1]
        return summed(back_to_columns(correlated(amp)))

    pull0, amp_pull = amplitudes([pull0_part, *sent(pull0_part)])
    beside_parts, cov_push_part = back_to_columns_early(correlated(amp_early), pull2_parts)
    cov_push = summed(cov_push_part)
    push_feed, push_state = mixtures(cov_push, [(down @ earlier @ later, first, ()), (earlier @ later, (), ())])
    rhs_feed, rhs_state = mixtures(rhs, [(down @ earlier, first, ()), (earlier, (), ())])
    fed = tangent(rhs_feed, push_feed)
    beside = summed_own(beside_parts)
    cov_start, pull2 = beside[:rows], beside[rows:]

    cov_pull = summed(back_to_columns(correlated(amp_pull)))
    pull_feed, pull_state = mixtures(
        cov_pull, [(down @ earlier @ later @ up, first, first), (earlier @ later @ up, (), first)]
    )
    fed_pull = tangent(pull_feed)
    pull0_fed, pull0_later, pull_next = mixtures(
        pull0, [(later @ up, first, first), (later @ up, (), first), (up, (), first)]
    )

    moved = fed[:rows] - fed_pull
    moved_turn = fed_pull + fed[rows:]
    turn_mult = plus(pull0_later, push_later)
    pull1 = None
    if pull0_fed is not None:
        pull1 = summed(adjoint(pull0_fed))
        pull1_fed, pull1_later, pull1_next = mixtures(
            pull1, [(later @ up, first, first), (later @ up, (), first), (up, (), first)]
        )
        pull2 = pull2 + own(summed(adjoint(pull0_fed - pull1_fed)))
        turn_mult = turn_mult - pull1_later
        cov_pull1 = covariance_sum(pull1)
        pull1_feed, pull1_state = mixtures(
            cov_pull1, [(down @ earlier @ later @ up, first, first), (earlier @ later @ up, (), first)]
        )
        push_state = push_state - pull1_state
        moved_turn = moved_turn - tangent(pull1_feed)
    moved_feed, moved_state = mixtures(moved, [(down @ earlier, first, first), (earlier, (), first)])
    if moved_feed is not None:
        moved_turn = moved_turn + tangent(joined(moved_feed))
    (next_pair,) = mixtures(jnp.concatenate([own(start), pull2], axis=0), [(up, (), ())])

    def inner_products(
        place_ref, rhs_ref, cov_start_ref, moved_ref, moved_turn_ref, moved_state_ref, data_ref, variance_ref,
        pick_ref, mine_ref, rhs_state_ref, pull_state_ref, push_state_ref, start_ref, push_ref,
        next_ref, pull_next_ref, *rest,
    ):
        sums_ref = rest[-1]
        moved = moved_ref[...]
        pull_own = own_rows(place_ref, pull_state_ref)
        state = own_rows(place_ref, rhs_state_ref) - pull_own
        turn_state = moved_state_ref[...] + pull_own + own_rows(place_ref, push_state_ref)
        res1 = own_rows(place_ref, rhs_ref) - cov_start_ref[...]
        image1 = res1 - moved
        turn1 = image1 - moved + moved_turn_ref[...]
        mine = mine_ref[...]
        chosen = own_rows(place_ref, pick_ref)
        res2 = data_ref[...] * mine
        seen = seen_by(chosen, state)
        image2 = res2 + seen
        turn2 = image2 + seen - seen_by(chosen, turn_state)
        push = own_rows(place_ref, push_ref)
        from_next = next_ref[:rows] - own_rows(place_ref, start_ref)
        res3 = from_next + own_rows(place_ref, pull_next_ref)
        step_next = own_rows(place_ref, pull_next_ref)
        for pull1_next_ref in rest[:-1]:
            step_next = step_next - own_rows(place_ref, pull1_next_ref)
        image3 = res3 + step_next + push
        turn3 = image3 + step_next - next_ref[rows:] + push + picked(seen / variance_ref[...], chosen)
        res = (res1, res2, res3)
        image = (image1, image2, image3)
        turn = (turn1, turn2, turn3)
        lane = lax.broadcasted_iota(jnp.int32, sums_ref.shape, 1)
        sums = jnp.zeros(sums_ref.shape, F32)
        for i, (left, right) in enumerate(((image, res), (image, image), (turn, res), (turn, image), (turn, turn))):
            value = sum(jnp.sum(a * b) for a, b in zip(left, right))
            sums = jnp.where(lane == i, value, sums)
        sums_ref[...] = sums

    everyone = ("sub", "col", "grp")
    devices = subs * shards * groups
    sums = call(
        inner_products,
        shape(devices, 128),
        [
            place, rhs, cov_start, moved, moved_turn, moved_state, data, variance, pick, mine,
            rhs_state, pull_state, push_state, start, push, next_pair, pull_next,
            *([] if pull1 is None else [pull1_next]),
        ],
        1000000,
    )
    sums = lax.all_to_all(sums, everyone, 0, 0, tiled=True)
    moved_state = joined(moved_state)

    def closing(
        sums_ref, start_ref, pull_later_ref, turn_mult_ref, data_ref, variance_ref, pick_ref,
        rhs_state_ref, pull_state_ref, push_state_ref, moved_state_ref, mult_ref, obs_ref, inc_ref,
    ):
        totals = jnp.sum(sums_ref[...], axis=0, keepdims=True)
        upper, square, turn_res, turn_image, turn_square = (totals[:, i : i + 1] for i in range(5))
        alpha = upper / square
        alpha_next = (upper - alpha * square - alpha * (turn_res - alpha * turn_image)) / (
            square - 2.0 * alpha * turn_image + alpha * alpha * turn_square
        )
        keep = alpha + alpha_next * (1.0 - alpha)
        mixed = alpha * alpha_next
        start_t = start_ref[...]
        state = rhs_state_ref[...] - pull_state_ref[...]
        turn_state = moved_state_ref[...] + pull_state_ref[...] + push_state_ref[...]
        mult_ref[...] = (start_t + keep * (pull_later_ref[...] - start_t) - mixed * turn_mult_ref[...]).T
        inc_ref[...] = (keep * state + mixed * turn_state).T
        seen = seen_by(pick_ref[...], state)
        data_t = data_ref[...]
        obs_ref[...] = ((alpha + alpha_next) * data_t - mixed * (data_t + seen)) / variance_ref[...]

    multiplier, obs_multiplier, increment = call(
        closing,
        [shape(depth, width), shape(slots, depth), shape(depth, width)],
        [
            sums, start, pull0_later, turn_mult, data, variance, pick,
            rhs_state, pull_state, push_state, moved_state,
        ],
        1000000,
    )
    return (multiplier[None], obs_multiplier[None], increment[None])


def solution(mesh):
    placed = (
        P("sub", None, "col"),
        P("sub", "col", None),
        P("sub", None, "col"),
        P("sub", None, "col"),
        P("grp", None),
        P(None, "grp"),
        P("grp", None),
        P(),
        P(),
        P("sub", "col"),
        P("sub", "col"),
        P("sub", "col"),
    )
    return jax.shard_map(
        on_device,
        mesh=mesh,
        in_specs=placed,
        out_specs=(P("sub", None, "col"), P("sub", "col", None), P("sub", None, "col")),
        check_vma=False,
    )
```

```python
import math

import jax
import jax.numpy as jnp
import numpy as np
from jax import lax
from jax.experimental import pallas as pl
from jax.experimental.pallas import tpu as pltpu
from jax.sharding import PartitionSpec as P

KW = 128


F32 = jnp.float32
BF16 = jnp.bfloat16


def spectrum(scales, limits, total, count):
    waves = jnp.arange(count, dtype=jnp.int32)
    wavef = waves.astype(jnp.float32)
    decay = jnp.exp(-0.5 * (2.0 * math.pi * wavef[None, :] * scales[:, None] / total) ** 2)
    factor = jnp.where(waves == 0, 1.0, 2.0).astype(jnp.float32) / total
    keep = (waves[None, :] < limits[:, None]).astype(jnp.float32)
    values = decay * factor[None, :] * keep
    return jnp.concatenate([values, values], axis=1)


def spectral_table(count, coarse, fine, origin):
    total = coarse * fine

    def small(columns):
        phase = (columns[:, None] + origin) * jnp.arange(count, dtype=jnp.int32)[None, :] % total
        angle = 2.0 * math.pi / total * phase.astype(F32)
        return jnp.cos(angle), jnp.sin(angle)

    cos_a, sin_a = (t[:, None, :] for t in small(jnp.arange(coarse, dtype=jnp.int32) * fine))
    cos_b, sin_b = (t[None, :, :] for t in small(jnp.arange(fine, dtype=jnp.int32)))
    table = jnp.concatenate([cos_a * cos_b - sin_a * sin_b, sin_a * cos_b + cos_a * sin_b], axis=2)
    return table.reshape(total, 2 * count)


def rotated(block, axis, distance):
    size = lax.axis_size(axis)
    return lax.ppermute(block, axis, [(i, (i + distance) % size) for i in range(size)])


def mixtures(field, plans):
    size = lax.axis_size("sub")
    here = lax.axis_index("sub")
    masked = []
    for matrix, unread, zero in plans:
        weights = np.array(matrix, dtype=np.float32)
        live = np.ones_like(weights, dtype=bool)
        live[list(unread), :] = False
        live[:, list(zero)] = False
        masked.append((weights, live))
    arrived = {0: field}
    cells = {0: [(i, i) for i in range(size)]}
    for distance in range(1, size):
        steps = [((source + distance) % size, source) for source in range(size)]
        cells[distance] = [c for c in steps if any(w[c] * l[c] for w, l in masked)]
        if cells[distance]:
            arrived[distance] = lax.ppermute(field, "sub", [(source, dest) for dest, source in cells[distance]])
    results = []
    for weights, live in masked:
        total = None
        for distance, block in arrived.items():
            used = {float(weights[c]) for c in cells[distance] if live[c]}
            if not used or used == {0.0}:
                continue
            if len(used) > 1:
                block = block * sum(
                    float(weights[dest, source]) * (here == dest).astype(F32) for dest, source in cells[distance]
                )
            elif used != {1.0}:
                block = block * used.pop()
            total = block if total is None else total + block
        results.append(total)
    return results


def plus(*terms):
    kept = [term for term in terms if term is not None]
    return sum(kept[1:], kept[0]) if kept else None


def halves(value):
    high = value.astype(BF16)
    return high, (value - high.astype(F32)).astype(BF16)


def contract(left, right, over):
    return lax.dot_general(left, right, (((over[0],), (over[1],)), ((), ())), preferred_element_type=F32)


def contract3(left, right, over):
    left_high, left_low = left
    right_high, right_low = right
    return (
        contract(left_high, right_low, over)
        + contract(left_low, right_high, over)
        + contract(left_high, right_high, over)
    )


def mixed_rows(left, right, fine, over):
    high, low = left
    right_high, right_low = right
    if high.shape[0] == fine:
        return contract3(left, right, over)
    wide = contract(jnp.concatenate([high, low], axis=0), right_high, over)
    exact = wide[:fine] + wide[high.shape[0] :] + contract(high[:fine], right_low, over)
    return jnp.concatenate([exact, wide[fine : high.shape[0]]], axis=0)


def fine_low(value, fine):
    high = value.astype(BF16)
    return high, (value[:fine] - high[:fine].astype(F32)).astype(BF16)


def call(kernel, out, inputs, flops, vmem_mib=16, grid=None, in_specs=None, out_specs=None, scratch=()):
    vmem = pl.BlockSpec(memory_space=pltpu.VMEM)
    smem = pl.BlockSpec(memory_space=pltpu.SMEM)
    if in_specs is None:
        in_specs = [smem if jnp.issubdtype(x.dtype, jnp.integer) else vmem for x in inputs]
        out_specs = jax.tree.map(lambda _: vmem, out)
    size = sum(math.prod(x.shape) * x.dtype.itemsize for x in [*inputs, *jax.tree.leaves(out)])
    return pl.pallas_call(
        kernel,
        out_shape=out,
        grid=grid or (),
        in_specs=in_specs,
        out_specs=out_specs,
        scratch_shapes=scratch,
        cost_estimate=pl.CostEstimate(flops=flops, bytes_accessed=size, transcendentals=0),
        compiler_params=pltpu.CompilerParams(vmem_limit_bytes=vmem_mib * 1024 * 1024),
    )(*inputs)


def shape(*dims):
    return jax.ShapeDtypeStruct(dims, F32)


def on_device(
    first_rhs,
    innovations,
    start_mult,
    trajectory,
    weight_in,
    weight_out,
    vertical_modes,
    length_scale,
    band_limit,
    obs_col,
    obs_count,
    obs_var,
):
    data = innovations[0]
    variance = obs_var[0][:, None]
    depth, width = first_rhs.shape[1:]
    slots = data.shape[0]
    subs = lax.axis_size("sub")
    shards = lax.axis_size("col")
    groups = lax.axis_size("grp")
    here = lax.axis_index("sub")
    column_index = lax.axis_index("col")
    group_index = lax.axis_index("grp")
    total_cols = width * shards
    hidden = weight_in.shape[0]
    half_modes = vertical_modes.shape[0]
    owned_modes = half_modes // shards
    rows = width // groups
    steps = 4
    block = hidden // steps

    ones = np.ones((subs, subs))
    up = np.eye(subs, k=1)
    down = np.eye(subs, k=-1)
    later = np.triu(ones)
    earlier = np.tril(ones)
    first = (0,)
    place = jnp.stack([group_index, here]).astype(jnp.int32)

    def turned(place_ref, outs, value):
        for step, ref in enumerate(outs):
            ref[...] = value_rows(value, lax.rem(place_ref[0] + step, groups))

    def value_rows(value, index):
        total = value[:rows]
        for other in range(1, groups):
            total = jnp.where(index == other, value[other * rows : (other + 1) * rows], total)
        return total

    def own_rows(place_ref, ref):
        return ref[pl.ds(pl.multiple_of(place_ref[0] * rows, rows), rows), :]

    def own(field):
        return lax.dynamic_slice_in_dim(field, group_index * rows, rows, 0)

    def sent(partial):
        return [rotated(partial, "grp", step) for step in range(1, groups)]

    def summed_own(parts):
        return plus(parts[0], *(rotated(parts[step], "grp", step) for step in range(1, groups)))

    def summed(partial):
        return plus(partial, *sent(partial))

    def joined(part):
        whole = lax.dynamic_update_slice_in_dim(jnp.zeros((width, depth), F32), part, group_index * rows, 0)
        for step in range(1, groups):
            source = (group_index - step) % groups
            whole = lax.dynamic_update_slice_in_dim(whole, rotated(part, "grp", step), source * rows, 0)
        return whole

    before = lax.ppermute(trajectory[0].astype(F32), "sub", [(i, i + 1) for i in range(subs - 1)])

    local_cols = obs_col[0] - column_index * width
    live = (jnp.arange(slots, dtype=jnp.int32) < obs_count[0, 0]).astype(F32)
    pick = (jnp.arange(width, dtype=jnp.int32)[:, None] == local_cols[None, :]).astype(F32)
    mine = ((local_cols // rows) == group_index).astype(F32)[:, None]
    pick = pick * live[None, :]

    def picked(values, chosen):
        high, low = halves(values)
        chosen = chosen.astype(BF16)
        return contract(chosen, high, (1, 0)) + contract(chosen, low, (1, 0))

    def seen_by(chosen, field):
        high, low = halves(field)
        chosen = chosen.astype(BF16)
        return contract(chosen, high, (0, 0)) + contract(chosen, low, (0, 0))

    def opening(start_ref, rhs_ref, data_ref, variance_ref, pick_ref, modes_ref, start_out, push_out, rhs_out, amp_ref):
        start_t = start_ref[...].T
        push_t = picked(data_ref[...] / variance_ref[...], pick_ref[...])
        start_out[...] = start_t
        push_out[...] = push_t
        rhs_out[...] = rhs_ref[...].T
        modes = halves(modes_ref[...])
        amp_ref[:, :width] = contract(modes[0], start_t.astype(BF16), (1, 1))
        amp_ref[:, width:] = contract3(modes, halves(push_t), (1, 1))

    start, push, rhs, amp_early = call(
        opening,
        [shape(width, depth)] * 3 + [shape(half_modes, 2 * width)],
        [start_mult[0], first_rhs[0], data, variance, pick, vertical_modes],
        8 * half_modes * depth * width,
    )
    weights = [pltpu.with_memory_space_constraint(w, pltpu.HBM) for w in (weight_in, weight_out)]
    whole_spec = [pl.BlockSpec(memory_space=pltpu.SMEM)]

    def fixed(*dims):
        return pl.BlockSpec(dims, lambda i: (0,) * len(dims))

    in_block = pl.BlockSpec((block, depth), lambda i: (i, 0))
    out_block = pl.BlockSpec((depth, block), lambda i: (0, i))
    slope_block = pl.BlockSpec((width, block), lambda i: (0, i))

    def slopes_and_adjoint(place_ref, fine_ref, rough_ref, before_ref, win_ref, wout_ref, fine_out, *rest):
        rough_outs, (slopes_ref, total_ref, turned_ref) = rest[:groups], rest[groups:]
        index = pl.program_id(0)

        @pl.when(index == 0)
        def _():
            total_ref[...] = jnp.zeros_like(total_ref)
            turned_ref[...] = before_ref[...].T.astype(BF16)

        win = halves(win_ref[...])
        wout = halves(wout_ref[...])
        state = turned_ref[...]
        bend = jnp.tanh(contract(state, win[1], (1, 1)) + contract(state, win[0], (1, 1)))
        slopes = (1.0 - bend * bend) * (place_ref[1] > 0).astype(F32)
        slopes_ref[...] = slopes
        fields = fine_low(jnp.concatenate([fine_ref[...], rough_ref[...]], axis=0), width)
        inner = mixed_rows(fields, wout, width, (1, 0)) * jnp.concatenate([slopes, slopes], axis=0)
        total_ref[...] += mixed_rows(fine_low(inner, width), win, width, (1, 0))

        @pl.when(index == steps - 1)
        def _():
            fine_out[...] = total_ref[:width]
            turned(place_ref, rough_outs, total_ref[width:])

    push_fed, push_later = mixtures(push, [(later, first, ()), (later, (), ())])
    pull0_part, *pull2_parts, slopes = call(
        slopes_and_adjoint,
        [shape(width, depth)] + [shape(rows, depth)] * groups + [shape(width, hidden)],
        [place, start, push_fed, before, *weights],
        20 * hidden * depth * width,
        vmem_mib=20,
        grid=(steps,),
        in_specs=whole_spec + [fixed(width, depth)] * 2 + [fixed(depth, width), in_block, out_block],
        out_specs=[fixed(width, depth)] + [fixed(rows, depth)] * groups + [slope_block],
        scratch=[pltpu.VMEM((2 * width, depth), F32), pltpu.VMEM((width, depth), BF16)],
    )

    def adjoint(field):
        def kernel(field_ref, slopes_ref, win_ref, wout_ref, total_ref):
            @pl.when(pl.program_id(0) == 0)
            def _():
                total_ref[...] = jnp.zeros_like(total_ref)

            inner = contract3(halves(field_ref[...]), halves(wout_ref[...]), (1, 0)) * slopes_ref[...]
            total_ref[...] += contract3(halves(inner), halves(win_ref[...]), (1, 0))

        return call(
            kernel,
            shape(width, depth),
            [field, slopes, *weights],
            12 * hidden * depth * width,
            vmem_mib=20,
            grid=(steps,),
            in_specs=[fixed(width, depth), slope_block, in_block, out_block],
            out_specs=fixed(width, depth),
        )

    def tangent(fine, rough=None):
        count = 1 if rough is None else 2

        def kernel(place_ref, *refs):
            fields, (slopes_ref, win_ref, wout_ref, *outs, total_ref) = refs[:count], refs[count:]

            @pl.when(pl.program_id(0) == 0)
            def _():
                total_ref[...] = jnp.zeros_like(total_ref)

            both = fine_low(jnp.concatenate([r[...] for r in fields], axis=0), width)
            slope = slopes_ref[...]
            inner = mixed_rows(both, halves(win_ref[...]), width, (1, 1)) * jnp.concatenate([slope] * count, axis=0)
            total_ref[...] += mixed_rows(fine_low(inner, width), halves(wout_ref[...]), width, (1, 1))

            @pl.when(pl.program_id(0) == steps - 1)
            def _():
                for i in range(count):
                    turned(
                        place_ref,
                        [out.at[i * rows : (i + 1) * rows] for out in outs],
                        total_ref[i * width : (i + 1) * width],
                    )

        parts = call(
            kernel,
            [shape(count * rows, depth)] * groups,
            [place, fine, *([] if rough is None else [rough]), slopes, *weights],
            (12 if rough is None else 16) * hidden * depth * width,
            vmem_mib=20,
            grid=(steps,),
            in_specs=whole_spec + [fixed(width, depth)] * count + [slope_block, in_block, out_block],
            out_specs=[fixed(count * rows, depth)] * groups,
            scratch=[pltpu.VMEM((count * width, depth), F32)],
        )
        return summed_own(parts)

    seed, amp_early = lax.optimization_barrier((place[0], amp_early))
    seed = seed - group_index
    first_mode = group_index * half_modes + column_index * owned_modes + seed
    owned_scales = lax.dynamic_slice_in_dim(length_scale, first_mode, owned_modes, 0)
    owned_limits = lax.dynamic_slice_in_dim(band_limit, first_mode, owned_modes, 0)
    owned_spec = spectrum(owned_scales, owned_limits, total_cols, KW)
    fine_cols = 1 << (total_cols.bit_length() // 2)
    table = spectral_table(KW, total_cols // fine_cols, fine_cols, seed)

    def amplitudes(field_parts):
        def kernel(*refs):
            modes_ref, whole_ref, amp_ref = refs[-3:]
            whole = plus(*(r[...] for r in refs[:-3]))
            whole_ref[...] = whole
            amp_ref[...] = contract3(halves(modes_ref[...]), halves(whole), (1, 1))

        return call(
            kernel,
            [shape(width, depth), shape(half_modes, width)],
            [*field_parts, vertical_modes],
            6 * half_modes * depth * width,
        )

    def correlated(amp):
        count = amp.shape[1] // width
        owned = lax.all_to_all(amp.reshape(shards, owned_modes, count * width), "col", 0, 0, tiled=True)

        def kernel(owned_ref, table_ref, spec_ref, back_ref):
            parts = halves(table_ref[...])
            for i in range(count):
                lanes = slice(i * width, (i + 1) * width)
                modes = jnp.concatenate([owned_ref[c][:, lanes] for c in range(shards)], axis=1)
                coeffs = contract3(halves(modes), parts, (1, 0)) * spec_ref[...]
                back = contract3(halves(coeffs), parts, (1, 1))
                for c in range(shards):
                    back_ref[c, :, lanes] = back[:, c * width : (c + 1) * width]

        back = call(
            kernel, shape(*owned.shape), [owned, table, owned_spec], 12 * owned_modes * count * total_cols * 2 * KW
        )
        returned = lax.all_to_all(back, "col", 0, 0, tiled=True)
        return returned.reshape(half_modes, count * width)

    def back_to_columns(returned):
        def kernel(returned_ref, modes_ref, out_ref):
            out_ref[...] = contract3(halves(returned_ref[...].T), halves(modes_ref[...]), (1, 0))

        return call(kernel, shape(width, depth), [returned, vertical_modes], 6 * half_modes * depth * width)

    def back_to_columns_early(returned, beside):
        def kernel(place_ref, returned_ref, modes_ref, *refs):
            beside_refs, rough_outs, fine_out = refs[:groups], refs[groups:-1], refs[-1]
            modes = halves(modes_ref[...])
            back = returned_ref[...].T
            rough = contract(back[:width].astype(BF16), modes[0], (1, 0))
            turned(place_ref, [out.at[:rows] for out in rough_outs], rough)
            for beside_ref, out in zip(beside_refs, rough_outs):
                out[rows:] = beside_ref[...]
            fine_out[...] = contract3(halves(back[width:]), modes, (1, 0))

        return call(
            kernel,
            [shape(2 * rows, depth)] * groups + [shape(width, depth)],
            [place, returned, vertical_modes, *beside],
            8 * half_modes * depth * width,
        )

    def covariance_sum(field):
        amp = amplitudes([field])[1]
        return summed(back_to_columns(correlated(amp)))

    pull0, amp_pull = amplitudes([pull0_part, *sent(pull0_part)])
    *beside_parts, cov_push_part = back_to_columns_early(correlated(amp_early), pull2_parts)
    cov_push = summed(cov_push_part)
    push_feed, push_state = mixtures(cov_push, [(down @ earlier @ later, first, ()), (earlier @ later, (), ())])
    rhs_feed, rhs_state = mixtures(rhs, [(down @ earlier, first, ()), (earlier, (), ())])
    fed = tangent(rhs_feed, push_feed)
    beside = summed_own(beside_parts)
    cov_start, pull2 = beside[:rows], beside[rows:]

    cov_pull = summed(back_to_columns(correlated(amp_pull)))
    pull_feed, pull_state = mixtures(
        cov_pull, [(down @ earlier @ later @ up, first, first), (earlier @ later @ up, (), first)]
    )
    fed_pull = tangent(pull_feed)
    pull0_fed, pull0_later, pull_next = mixtures(
        pull0, [(later @ up, first, first), (later @ up, (), first), (up, (), first)]
    )

    moved = fed[:rows] - fed_pull
    moved_turn = fed_pull + fed[rows:]
    turn_mult = plus(pull0_later, push_later)
    pull1 = None
    if pull0_fed is not None:
        pull1 = summed(adjoint(pull0_fed))
        pull1_fed, pull1_later, pull1_next = mixtures(
            pull1, [(later @ up, first, first), (later @ up, (), first), (up, (), first)]
        )
        pull2 = pull2 + own(summed(adjoint(pull0_fed - pull1_fed)))
        turn_mult = turn_mult - pull1_later
        cov_pull1 = covariance_sum(pull1)
        pull1_feed, pull1_state = mixtures(
            cov_pull1, [(down @ earlier @ later @ up, first, first), (earlier @ later @ up, (), first)]
        )
        push_state = push_state - pull1_state
        moved_turn = moved_turn - tangent(pull1_feed)
    moved_feed, moved_state = mixtures(moved, [(down @ earlier, first, first), (earlier, (), first)])
    if moved_feed is not None:
        moved_turn = moved_turn + tangent(joined(moved_feed))
    (next_pair,) = mixtures(jnp.concatenate([own(start), pull2], axis=0), [(up, (), ())])

    def inner_products(
        place_ref, rhs_ref, cov_start_ref, moved_ref, moved_turn_ref, moved_state_ref, data_ref, variance_ref,
        pick_ref, mine_ref, rhs_state_ref, pull_state_ref, push_state_ref, start_ref, push_ref,
        next_ref, pull_next_ref, *rest,
    ):
        sums_ref = rest[-1]
        moved = moved_ref[...]
        pull_own = own_rows(place_ref, pull_state_ref)
        state = own_rows(place_ref, rhs_state_ref) - pull_own
        turn_state = moved_state_ref[...] + pull_own + own_rows(place_ref, push_state_ref)
        res1 = own_rows(place_ref, rhs_ref) - cov_start_ref[...]
        image1 = res1 - moved
        turn1 = image1 - moved + moved_turn_ref[...]
        mine = mine_ref[...]
        chosen = own_rows(place_ref, pick_ref)
        res2 = data_ref[...] * mine
        seen = seen_by(chosen, state)
        image2 = res2 + seen
        turn2 = image2 + seen - seen_by(chosen, turn_state)
        push = own_rows(place_ref, push_ref)
        from_next = next_ref[:rows] - own_rows(place_ref, start_ref)
        res3 = from_next + own_rows(place_ref, pull_next_ref)
        step_next = own_rows(place_ref, pull_next_ref)
        for pull1_next_ref in rest[:-1]:
            step_next = step_next - own_rows(place_ref, pull1_next_ref)
        image3 = res3 + step_next + push
        turn3 = image3 + step_next - next_ref[rows:] + push + picked(seen / variance_ref[...], chosen)
        res = (res1, res2, res3)
        image = (image1, image2, image3)
        turn = (turn1, turn2, turn3)
        lane = lax.broadcasted_iota(jnp.int32, sums_ref.shape, 1)
        sums = jnp.zeros(sums_ref.shape, F32)
        for i, (left, right) in enumerate(((image, res), (image, image), (turn, res), (turn, image), (turn, turn))):
            value = sum(jnp.sum(a * b) for a, b in zip(left, right))
            sums = jnp.where(lane == i, value, sums)
        sums_ref[...] = sums

    everyone = ("sub", "col", "grp")
    devices = subs * shards * groups
    sums = call(
        inner_products,
        shape(devices, 128),
        [
            place, rhs, cov_start, moved, moved_turn, moved_state, data, variance, pick, mine,
            rhs_state, pull_state, push_state, start, push, next_pair, pull_next,
            *([] if pull1 is None else [pull1_next]),
        ],
        1000000,
    )
    sums = lax.all_to_all(sums, everyone, 0, 0, tiled=True)
    moved_state = joined(moved_state)

    def closing(
        sums_ref, start_ref, pull_later_ref, turn_mult_ref, data_ref, variance_ref, pick_ref,
        rhs_state_ref, pull_state_ref, push_state_ref, moved_state_ref, mult_ref, obs_ref, inc_ref,
    ):
        totals = jnp.sum(sums_ref[...], axis=0, keepdims=True)
        upper, square, turn_res, turn_image, turn_square = (totals[:, i : i + 1] for i in range(5))
        alpha = upper / square
        alpha_next = (upper - alpha * square - alpha * (turn_res - alpha * turn_image)) / (
            square - 2.0 * alpha * turn_image + alpha * alpha * turn_square
        )
        keep = alpha + alpha_next * (1.0 - alpha)
        mixed = alpha * alpha_next
        start_t = start_ref[...]
        state = rhs_state_ref[...] - pull_state_ref[...]
        turn_state = moved_state_ref[...] + pull_state_ref[...] + push_state_ref[...]
        mult_ref[...] = (start_t + keep * (pull_later_ref[...] - start_t) - mixed * turn_mult_ref[...]).T
        inc_ref[...] = (keep * state + mixed * turn_state).T
        seen = seen_by(pick_ref[...], state)
        data_t = data_ref[...]
        obs_ref[...] = ((alpha + alpha_next) * data_t - mixed * (data_t + seen)) / variance_ref[...]

    multiplier, obs_multiplier, increment = call(
        closing,
        [shape(depth, width), shape(slots, depth), shape(depth, width)],
        [
            sums, start, pull0_later, turn_mult, data, variance, pick,
            rhs_state, pull_state, push_state, moved_state,
        ],
        1000000,
    )
    return (multiplier[None], obs_multiplier[None], increment[None])


def solution(mesh):
    placed = (
        P("sub", None, "col"),
        P("sub", "col", None),
        P("sub", None, "col"),
        P("sub", None, "col"),
        P("grp", None),
        P(None, "grp"),
        P("grp", None),
        P(),
        P(),
        P("sub", "col"),
        P("sub", "col"),
        P("sub", "col"),
    )
    return jax.shard_map(
        on_device,
        mesh=mesh,
        in_specs=placed,
        out_specs=(P("sub", None, "col"), P("sub", "col", None), P("sub", None, "col")),
        check_vma=False,
    )
```
